512 devices in a mesh: seq: 128 (over z_hi, y, x, core), chan: 4 (over z_lo).
Axes of the slice: x: 4, y: 8, z: 8 (z_hi: 2, z_lo: 4; z = z_hi * 4 + z_lo), core: 2. Of those that a mesh axis runs over, the one named last changes fastest.
Arguments:
- latent: bfloat16 [65536, 16], P(('seq', 'chan')), may hold values from -140 to 140
- in_weight: bfloat16 [9, 16, 384], P(None, 'chan'), may hold values from -2 to 2
- in_bias: float32 [384], P('chan'), may hold values from -1.75 to 1.75
- norm_gain: float32 [3, 2, 384], P(None, None, 'chan'), may hold values from 0.1 to 1.9
- norm_shift: float32 [3, 2, 384], P(None, None, 'chan'), may hold values from -1.75 to 1.75
- res_weight: bfloat16 [3, 2, 9, 384, 384], P(None, None, None, 'chan'), may hold values from -2 to 2
- res_bias: float32 [3, 2, 384], P(None, None, 'chan'), may hold values from -1.75 to 1.75
- up_weight: bfloat16 [9, 384, 192], P(None, 'chan'), may hold values from -0.109375 to 0.109375
- up_bias: float32 [192], P('chan'), may hold values from -1.75 to 1.75
Outputs:
- image: bfloat16 [192, 512, 512], P('chan', 'seq')
The draws below stay inside these ranges and needn't reach their ends.
All inputs are finite; a program needn't handle non-finite values.
Results may differ from the reference program's by a relative error of at most 0.022.
Values may be sent and summed in bfloat16 or wider, within the bound.
A program may use at most 64 MiB of HBM per device.

```python
import math
import jax
import jax.numpy as jnp
from jax import lax

LAT_C = 16
CH = 384
UP_CH = 192
LAYERS = 3
LAT_W = 256
HEIGHT = 256
TOKENS = 65536
N_CHAN = 4


def draw_latent(key, part):
    noise_key, token_key, chan_key = jax.random.split(key, 3)
    row_index = (jnp.arange(TOKENS, dtype=jnp.int32) // LAT_W).astype(jnp.float32)
    height_pos = row_index / max(HEIGHT - 1, 1)
    token_scale = jnp.exp(jax.random.uniform(token_key, (TOKENS,), jnp.float32, math.log(0.3), math.log(3.0)))
    chan_scale = jnp.exp(jax.random.uniform(chan_key, (LAT_C,), jnp.float32, math.log(0.5), math.log(2.0)))
    ramp = jnp.exp(math.log(3.0) * height_pos)
    base = jax.random.truncated_normal(noise_key, -4.0, 4.0, (TOKENS, LAT_C), jnp.float32)
    values = base * token_scale[:, None] * chan_scale[None, :] * ramp[:, None]
    return values.astype(jnp.bfloat16)


def rising_weight(key, shape, fan_in):
    noise_key, factor_key = jax.random.split(key, 2)
    outputs = shape[-1]
    position = jnp.arange(outputs, dtype=jnp.int32).astype(jnp.float32) / max(outputs - 1, 1)
    factor = jnp.exp(jax.random.uniform(factor_key, (outputs,), jnp.float32, math.log(0.7), math.log(1.4)))
    ramp = jnp.exp(math.log(8.0) * (position - 0.5))
    base = jax.random.truncated_normal(noise_key, -4.0, 4.0, shape, jnp.float32)
    return base * (ramp * factor) * fan_in ** (-0.5)


def draw_in_weight(key, part):
    values = rising_weight(jax.random.fold_in(key, 11), (9, LAT_C, CH), 9.0 * LAT_C)
    return values.astype(jnp.bfloat16)


def draw_res_weight(key, part):
    values = rising_weight(jax.random.fold_in(key, 23), (LAYERS, 2, 9, CH, CH), 9.0 * CH)
    return values.astype(jnp.bfloat16)


def block_levels(key, extent, cuts, least, high):
    loudness = 1.0
    for axis_at, parts in cuts:
        heights = jax.random.uniform(jax.random.fold_in(jax.random.fold_in(key, 6), axis_at), (parts,), jnp.float32, least / len(cuts), high / len(cuts))
        loudness = loudness * jnp.repeat(jnp.exp(heights), extent[axis_at] // parts).reshape((-1,) + (1,) * (len(extent) - 1 - axis_at))
    return loudness


def scatter_about(stream_key, shape, spread, limit, cuts=(), kind=jnp.bfloat16):
    array = jax.random.normal(stream_key, shape, jnp.float32) * spread
    if len(cuts) > 0:
        array = block_levels(stream_key, shape, cuts, -0.22, 0.18) * array
    return jnp.clip(array, min=-limit, max=limit).astype(kind)


def setup_inputs(seed: int = 0) -> dict:
    streams_of = jax.random.split(jax.random.key(seed), 10)
    latent = draw_latent(jax.random.fold_in(streams_of[9], 71), 0)
    in_weight = draw_in_weight(jax.random.fold_in(streams_of[9], 71), 0)
    in_bias = scatter_about(streams_of[2], (CH,), 0.3, 1.75, ((0, 4),), jnp.float32)
    norm_gain = jnp.clip(1.0 + 0.18 * jax.random.normal(streams_of[3], (LAYERS, 2, CH), jnp.float32), 0.1, 1.9)
    norm_shift = scatter_about(streams_of[4], (LAYERS, 2, CH), 0.3, 1.75, ((2, 4),), jnp.float32)
    res_weight = draw_res_weight(jax.random.fold_in(streams_of[9], 71), 0)
    res_bias = scatter_about(streams_of[6], (LAYERS, 2, CH), 0.3, 1.75, ((2, 4),), jnp.float32)
    up_weight = scatter_about(streams_of[7], (9, CH, UP_CH), (9 * CH) ** -0.5, 0.109375, ((1, 4),))
    up_bias = scatter_about(streams_of[8], (UP_CH,), 0.3, 1.75, ((0, 4),), jnp.float32)
    return dict(latent=latent, in_weight=in_weight, in_bias=in_bias, norm_gain=norm_gain, norm_shift=norm_shift, res_weight=res_weight, res_bias=res_bias, up_weight=up_weight, up_bias=up_bias)


EPS = 1e-06

def conv_sum(values, weight, bias):
    chans, height, width = values.shape
    outputs = weight.shape[2]
    quarter = chans // N_CHAN
    padded = jnp.pad(values, ((0, 0), (1, 1), (1, 1)))

    def quarter_sum(index):
        block = lax.dynamic_slice_in_dim(padded, index * quarter, quarter, 0).astype(jnp.float32)
        taps = lax.dynamic_slice_in_dim(weight, index * quarter, quarter, 1).astype(jnp.float32)
        totals = jnp.zeros((outputs, height * width), jnp.float32)
        for tap_index in range(9):
            row_off = tap_index // 3
            col_off = tap_index % 3
            window = block[:, row_off:row_off + height, col_off:col_off + width].reshape(quarter, height * width)
            totals = totals + jnp.dot(taps[tap_index].T, window, preferred_element_type=jnp.float32)
        return totals.astype(jnp.bfloat16)
    pieces = lax.map(quarter_sum, jnp.arange(N_CHAN, dtype=jnp.int32))
    summed = lax.optimization_barrier(jnp.sum(pieces.astype(jnp.float32), axis=0)) + bias[:, None]
    return summed.reshape(outputs, height, width)

def rms_norm(values, gain_vec, shift_vec):
    mean_sq = lax.optimization_barrier(jnp.mean(values * values, axis=0, keepdims=True))
    normed = values * lax.rsqrt(mean_sq + EPS)
    return normed * gain_vec[:, None, None] + shift_vec[:, None, None]

def reference(latent, in_weight, in_bias, norm_gain, norm_shift, res_weight, res_bias, up_weight, up_bias):
    slab_field = latent.T.reshape(LAT_C, HEIGHT, LAT_W)
    stream = conv_sum(slab_field, in_weight, in_bias).astype(jnp.bfloat16)
    for layer_idx in range(LAYERS):
        normed = jax.nn.silu(rms_norm(stream.astype(jnp.float32), norm_gain[layer_idx, 0], norm_shift[layer_idx, 0])).astype(jnp.bfloat16)
        middle = conv_sum(normed, res_weight[layer_idx, 0], res_bias[layer_idx, 0])
        branch_in = jax.nn.silu(rms_norm(middle, norm_gain[layer_idx, 1], norm_shift[layer_idx, 1])).astype(jnp.bfloat16)
        stream = (stream.astype(jnp.float32) + conv_sum(branch_in, res_weight[layer_idx, 1], res_bias[layer_idx, 1])).astype(jnp.bfloat16)
    widened = jnp.repeat(jnp.repeat(stream, 2, axis=1), 2, axis=2)
    return conv_sum(widened, up_weight, up_bias).astype(jnp.bfloat16)
```

```python
import jax
import jax.numpy as jnp
from jax import lax
from jax.experimental import pallas as pl
from jax.experimental.pallas import tpu as pltpu
from jax.sharding import PartitionSpec as P

CH = 384
UP = 192
EPS = 1e-06
COLS = 80
NRES = 54
NPIECE = 63
LAG = 8
MESH = pl.DeviceIdType.MESH


def remote(src, dst, send_sem, recv_sem, device):
    return pltpu.make_async_remote_copy(
        src_ref=src,
        dst_ref=dst,
        send_sem=send_sem,
        recv_sem=recv_sem,
        device_id=device,
        device_id_type=MESH,
    )


def kernel(
    lat_in, win_in, ibias_in, gain_in, shift_in, wres_in, rbias_in, wup_in, ubias_in,
    out_ref,
    lat_buf, win_buf, ibias_buf, gain_buf, shift_buf, rbias_buf, ubias_buf,
    wbuf, ubuf, table, lrow, win, x3, hbuf, upx, obuf,
    lat_s, lat_r, small_s, small_r, loc, zs, xs, ys, ps, r1, r2, out_s, out_r,
):
    s = lax.axis_index("seq")
    c = lax.axis_index("chan")
    core = lax.rem(s, 2)
    x = lax.rem(lax.div(s, 2), 4)
    y = lax.rem(lax.div(s, 8), 8)
    zh = lax.div(s, 64)
    z = zh * 4 + c
    bx, by = lax.rem(x, 2), lax.rem(y, 2)
    partner = (s + 1 - 2 * core, c)

    def z_device(step):
        zz = lax.rem(z + 8 + step, 8)
        return (((lax.div(zz, 4) * 8 + y) * 4 + x) * 2 + core, lax.rem(zz, 4))

    def x_device(step):
        xx = lax.rem(x + 4 + step, 4)
        return (((zh * 8 + y) * 4 + xx) * 2 + core, c)

    def y_device(step):
        yy = lax.rem(y + 8 + step, 8)
        return (((zh * 8 + yy) * 4 + x) * 2 + core, c)

    barrier = pltpu.get_barrier_semaphore()
    others = []
    for ds in range(-4, 5):
        peer = lax.rem(s + 128 + ds, 128)
        for dc in range(4):
            if ds != 0 or dc != 0:
                others.append((peer, lax.rem(c + dc, 4)))
    for step in (-2, -1, 1, 2):
        others.append(z_device(step))
    for step in (-1, 1):
        others.append(x_device(step))
        others.append(y_device(step))
    for device in others:
        pl.semaphore_signal(barrier, inc=1, device_id=device, device_id_type=MESH)
    for k in range(6):
        pltpu.make_async_copy(
            wres_in.at[k // 2, k % 2], wbuf.at[k, :, pl.ds(c * 96, 96), :], loc.at[k]
        ).start()
    pltpu.make_async_copy(wup_in, ubuf.at[:, pl.ds(c * 96, 96), :], loc.at[6]).start()
    pl.semaphore_wait(barrier, len(others))

    def lat_copy(ds, dc):
        return remote(
            lat_in,
            lat_buf.at[4 * (4 - ds) + c],
            lat_s.at[(ds + 4) * 4 + dc],
            lat_r.at[4 * (4 - ds) + c],
            (lax.rem(s + 128 + ds, 128), lax.rem(c + dc, 4)),
        )

    lat_pairs = [(ds, dc) for ds in range(-4, 5) for dc in range(4) if ds != 0 or dc != 0]
    for ds, dc in lat_pairs:
        lat_copy(ds, dc).start()
    pltpu.make_async_copy(lat_in, lat_buf.at[16 + c], loc.at[7]).start()
    smalls = (
        (win_in, win_buf),
        (ibias_in, ibias_buf),
        (gain_in, gain_buf),
        (shift_in, shift_buf),
        (rbias_in, rbias_buf),
        (ubias_in, ubias_buf),
    )

    def small_copy(i, dc):
        src, dst = smalls[i]
        return remote(
            src, dst.at[c], small_s.at[i * 4 + dc], small_r.at[i * 4 + c], (s, lax.rem(c + dc, 4))
        )

    for i in range(6):
        for dc in range(1, 4):
            small_copy(i, dc).start()
        pltpu.make_async_copy(smalls[i][0], smalls[i][1].at[c], loc.at[8 + i]).start()

    def res_piece(v, quarter):
        k, g = lax.div(v, 9), lax.div(lax.rem(v, 9), 3)
        return wbuf.at[k, pl.ds(3 * g, 3), pl.ds(quarter * 96 + core * 48, 48), :]

    def up_piece(v, quarter):
        g = lax.div(v - NRES, 3)
        return ubuf.at[pl.ds(3 * g, 3), pl.ds(quarter * 96 + core * 48, 48), :]

    def source_copy(v, up):
        which = lax.rem(v, 3)
        far = 4 * lax.rem(lax.div(v, 12), 2) - 2
        target = z_device(jnp.where(which == 0, -1, jnp.where(which == 2, 1, far)))
        if up:
            src = wup_in.at[pl.ds(3 * lax.div(v - NRES, 3), 3), pl.ds(core * 48, 48), :]
            dst = up_piece(v, c)
        else:
            k, g = lax.div(v, 9), lax.div(lax.rem(v, 9), 3)
            src = wres_in.at[
                lax.div(k, 2), lax.rem(k, 2), pl.ds(3 * g, 3), pl.ds(core * 48, 48), :
            ]
            dst = res_piece(v, c)
        return remote(src, dst, zs.at[v], r1.at[v], target)

    def is_source(v):
        chi = lax.rem(v, 4)
        return (lax.rem(chi, 2) == bx) & (lax.div(chi, 2) == by)

    for up, lo, hi in ((False, 0, NRES), (True, NRES, NPIECE)):

        @pl.loop(lo, hi)
        def _(v):
            @pl.when(is_source(v))
            def _():
                source_copy(v, up).start()

    def parts_of(v, up):
        piece = (up_piece if up else res_piece)(v, lax.rem(c + 1 + lax.rem(v, 3), 4))
        turn = 2 * lax.rem(lax.div(v, 8), 2) - 1
        return (
            remote(piece, piece, xs.at[v], r1.at[v], x_device(turn)),
            remote(piece, piece, ys.at[v], r1.at[v], y_device(turn)),
            remote(piece, piece, ps.at[v], r2.at[v], partner),
        )

    def role_of(v):
        chi, y_first = lax.rem(v, 4), lax.rem(lax.div(v, 4), 2)
        rx = lax.rem(bx + lax.rem(chi, 2), 2)
        ry = lax.rem(by + lax.div(chi, 2), 2)
        first = jnp.where(y_first == 1, rx, ry)
        second = jnp.where(y_first == 1, ry, rx)
        return jnp.where(first == 1, 2, second), y_first

    def pass_on(v, phase, up):
        role, y_first = role_of(v)
        low, high = (NRES, NPIECE) if up else (0, NRES)

        @pl.when((v >= low) & (v < high) & (role == phase))
        def _():
            along_x, along_y, across = parts_of(v, up)
            along_x.wait_recv()
            if phase == 0:
                along_x.start()
                along_y.start()
            if phase == 1:

                @pl.when(y_first == 1)
                def _():
                    along_x.start()

                @pl.when(y_first == 0)
                def _():
                    along_y.start()

            across.start()

    def relay(t):
        for phase in range(3):
            for up in (False, True):
                pass_on(t + (3 * LAG) - LAG * phase - 3 * LAG, phase, up)

    def relays(lo, hi):
        @pl.loop(lo, hi)
        def _(t):
            relay(t)

    ready = 9 + 2 * LAG
    relays(0, 6)

    for i in range(6):
        for dc in range(1, 4):
            src, dst = smalls[i]
            peer = lax.rem(c + dc, 4)
            remote(
                src, dst.at[peer], small_s.at[i * 4 + dc], small_r.at[i * 4 + peer], (s, peer)
            ).wait_recv()
        pltpu.make_async_copy(smalls[i][0], smalls[i][1].at[c], loc.at[8 + i]).wait()
    for q in range(4):
        for i in range(6):
            at = pl.ds(96 * q, 96)
            table[pl.ds(i, 1), at] = gain_buf[q, i // 2, pl.ds(i % 2, 1), :]
            table[pl.ds(6 + i, 1), at] = shift_buf[q, i // 2, pl.ds(i % 2, 1), :]
            table[pl.ds(12 + i, 1), at] = rbias_buf[q, i // 2, pl.ds(i % 2, 1), :]
        table[pl.ds(18, 1), pl.ds(96 * q, 96)] = ibias_buf[q]
        table[pl.ds(19, 1), pl.ds(48 * q, 48)] = ubias_buf[q]
    total = jnp.zeros((144, CH), jnp.float32)
    for q in range(4):
        row = lax.broadcasted_iota(jnp.int32, (144, 36), 0)
        col = lax.broadcasted_iota(jnp.int32, (144, 36), 1)
        put = (row == (col >> 2) * 16 + 4 * q + (col & 3)).astype(jnp.float32)
        total += jnp.dot(
            put.astype(jnp.bfloat16), win_buf[q], preferred_element_type=jnp.float32
        )
    win[...] = total.astype(jnp.bfloat16)

    for ds, dc in lat_pairs:
        slot = 4 * (4 - ds) + lax.rem(c + dc, 4)
        remote(lat_in, lat_buf.at[slot], lat_s.at[0], lat_r.at[slot], partner).wait_recv()
    pltpu.make_async_copy(lat_in, lat_buf.at[16 + c], loc.at[7]).wait()
    col_lo = jnp.maximum(8 - 64 * c, 0)
    col_hi = jnp.minimum(264 - 64 * c, COLS)
    turn = lax.rem(8 + 256 - 64 * c, 256)
    lane = lax.broadcasted_iota(jnp.int32, (16, 128), 1)

    @pl.loop(0, 18)
    def _(r):
        both = jnp.concatenate([lat_buf[2 * r], lat_buf[2 * r + 1]], axis=1).astype(jnp.float32)
        window = pltpu.roll(both, turn, 1)[:, :128]
        row = 2 * s - 8 + r
        top = jnp.where((row >= 0) & (row < 256), col_hi, 0)
        window = jnp.where((lane >= col_lo) & (lane < top), window, 0.0)
        at = pl.ds(pl.multiple_of(r * 16, 16), 16)
        lrow[0, at, :] = pltpu.roll(window, 1, 1).astype(jnp.bfloat16)
        lrow[1, at, :] = window.astype(jnp.bfloat16)
        lrow[2, at, :] = pltpu.roll(window, 127, 1).astype(jnp.bfloat16)

    pixel = lax.broadcasted_iota(jnp.int32, (COLS, CH), 0)

    def spread(dst, a, values):
        row = 2 * s - 7 + a
        top = jnp.where((row >= 0) & (row < 256), col_hi, 0)
        kept = jnp.where((pixel >= col_lo) & (pixel < top), values, 0.0)
        x3[dst, a, :, pl.ds(0, CH)] = pltpu.roll(kept, 1, 0).astype(jnp.bfloat16)
        x3[dst, a, :, pl.ds(CH, CH)] = kept.astype(jnp.bfloat16)
        x3[dst, a, :, pl.ds(2 * CH, CH)] = pltpu.roll(kept, COLS - 1, 0).astype(jnp.bfloat16)

    def normed(values, i):
        mean = jnp.sum(values * values, axis=1, keepdims=True) * (1.0 / CH)
        u = values * lax.rsqrt(mean + EPS) * table[pl.ds(i, 1), :] + table[pl.ds(6 + i, 1), :]
        half = 0.5 * u
        return half * jnp.tanh(half) + half

    def rounded(values):
        return values.astype(jnp.bfloat16).astype(jnp.float32)

    @pl.loop(0, 16)
    def _(i):
        columns = jnp.concatenate(
            [
                lrow[q, pl.ds(pl.multiple_of((i + p) * 16, 16), 16), :]
                for p in range(3)
                for q in range(3)
            ],
            axis=0,
        )
        acc = lax.dot_general(
            columns, win[...], (((0,), (0,)), ((), ())), preferred_element_type=jnp.float32
        )
        stream = rounded(acc[:COLS] + table[pl.ds(18, 1), :])
        hbuf[i] = stream
        spread(0, i, normed(stream, 0))
        relays(6 + lax.div(i * (ready - 6), 16), 6 + lax.div((i + 1) * (ready - 6), 16))

    for k in range(6):
        src, dst = k % 2, 1 - k % 2
        pltpu.make_async_copy(
            wres_in.at[k // 2, k % 2], wbuf.at[k, :, pl.ds(c * 96, 96), :], loc.at[k]
        ).wait()

        @pl.loop(9 * k, 9 * k + 9)
        def _(v):
            piece = wbuf.at[k, pl.ds(3 * lax.div(lax.rem(v, 9), 3), 3),
                            pl.ds(lax.rem(c + 1 + lax.rem(v, 3), 4) * 96 + (1 - core) * 48, 48), :]
            remote(piece, piece, ps.at[v], r2.at[v], partner).wait_recv()

        blocks = 7 - k

        @pl.loop(0, blocks)
        def _(b):
            a = k + 1 + 2 * b
            acc = jnp.zeros((2 * COLS, CH), jnp.float32)
            for p in range(3):
                acc += jnp.dot(
                    x3[src, pl.ds(a - 1 + p, 2)].reshape(2 * COLS, 3 * CH),
                    wbuf[k, pl.ds(3 * p, 3)].reshape(3 * CH, CH),
                    preferred_element_type=jnp.float32,
                )
            acc += table[pl.ds(12 + k, 1), :]
            for j in range(2):
                values = acc[j * COLS : (j + 1) * COLS]
                if k % 2 == 0:
                    spread(dst, a + j, normed(values, k + 1))
                else:
                    values = rounded(hbuf[a + j] + values)
                    hbuf[a + j] = values
                    spread(dst, a + j, normed(values, k + 1) if k < 5 else values)
            relays(ready + 9 * k + lax.div(b * 9, blocks), ready + 9 * k + lax.div((b + 1) * 9, blocks))

    pltpu.make_async_copy(wup_in, ubuf.at[:, pl.ds(c * 96, 96), :], loc.at[6]).wait()

    @pl.loop(NRES, NPIECE)
    def _(v):
        piece = ubuf.at[pl.ds(3 * lax.div(v - NRES, 3), 3),
                        pl.ds(lax.rem(c + 1 + lax.rem(v, 3), 4) * 96 + (1 - core) * 48, 48), :]
        remote(piece, piece, ps.at[v], r2.at[v], partner).wait_recv()

    def out_copy(r, dc):
        peer = lax.rem(c + dc, 4)
        return remote(
            obuf.at[r, pl.ds(peer * 48, 48), :],
            out_ref.at[r, :, pl.ds(c * 128, 128)],
            out_s.at[r * 4 + dc],
            out_r.at[r * 4 + c],
            (s, peer),
        )

    lanes = ((0, 1, 1), (1, 1, 2))
    rows = ((-1, 0, 0), (0, 0, 1))
    for i in range(2):
        for b2 in range(2):
            acc = jnp.zeros((2 * COLS, UP), jnp.float32)
            for p in range(3):
                lhs = jnp.concatenate(
                    [
                        jnp.concatenate(
                            [
                                x3[0, 7 + i + rows[a2][p], :, pl.ds(CH * lanes[b2][q], CH)]
                                for q in range(3)
                            ],
                            axis=1,
                        )
                        for a2 in range(2)
                    ],
                    axis=0,
                )
                acc += jnp.dot(
                    lhs,
                    ubuf[pl.ds(3 * p, 3)].reshape(3 * CH, UP),
                    preferred_element_type=jnp.float32,
                )
            acc += table[pl.ds(19, 1), pl.ds(0, UP)]
            for a2 in range(2):
                part = acc[a2 * COLS + 8 : a2 * COLS + 72]
                upx[a2, 0, pl.ds(b2, 64, stride=2), :] = part[:, :128]
                upx[a2, 1, pl.ds(b2, 64, stride=2), pl.ds(0, 64)] = part[:, 128:]
        for a2 in range(2):
            r = 2 * i + a2
            obuf[r, pl.ds(0, 128), :] = upx[a2, 0].T.astype(jnp.bfloat16)
            obuf[r, pl.ds(128, 64), :] = upx[a2, 1].T[:64].astype(jnp.bfloat16)
            for dc in range(1, 4):
                out_copy(r, dc).start()
            pltpu.make_async_copy(
                obuf.at[r, pl.ds(c * 48, 48), :],
                out_ref.at[r, :, pl.ds(c * 128, 128)],
                loc.at[14 + r],
            ).start()

    for r in range(4):
        for dc in range(1, 4):
            out_copy(r, dc).wait_send()
            peer = lax.rem(c + dc, 4)
            remote(
                obuf.at[r, pl.ds(0, 48), :],
                out_ref.at[r, :, pl.ds(peer * 128, 128)],
                out_s.at[r * 4 + dc],
                out_r.at[r * 4 + peer],
                (s, peer),
            ).wait_recv()
        pltpu.make_async_copy(
            obuf.at[r, pl.ds(c * 48, 48), :],
            out_ref.at[r, :, pl.ds(c * 128, 128)],
            loc.at[14 + r],
        ).wait()
    for ds, dc in lat_pairs:
        lat_copy(ds, dc).wait_send()
    for i in range(6):
        for dc in range(1, 4):
            small_copy(i, dc).wait_send()
    for up, lo, hi in ((False, 0, NRES), (True, NRES, NPIECE)):

        @pl.loop(lo, hi)
        def _(v):
            @pl.when(is_source(v))
            def _():
                source_copy(v, up).wait_send()

            role, y_first = role_of(v)
            along_x, along_y, across = parts_of(v, up)

            @pl.when((role == 0) | ((role == 1) & (y_first == 1)))
            def _():
                along_x.wait_send()

            @pl.when((role == 0) | ((role == 1) & (y_first == 0)))
            def _():
                along_y.wait_send()

            across.wait_send()


def body(
    latent, in_weight, in_bias, norm_gain, norm_shift, res_weight, res_bias, up_weight, up_bias
):
    bf16, f32 = jnp.bfloat16, jnp.float32
    dma = pltpu.SemaphoreType.DMA
    image = pl.pallas_call(
        kernel,
        out_shape=jax.ShapeDtypeStruct((4, 48, 512), bf16),
        in_specs=[pl.BlockSpec(memory_space=pl.ANY)] * 9,
        out_specs=pl.BlockSpec(memory_space=pltpu.VMEM),
        scratch_shapes=[
            pltpu.VMEM((36, 16, 128), bf16),
            pltpu.VMEM((4, 36, CH), bf16),
            pltpu.VMEM((4, 1, 96), f32),
            pltpu.VMEM((4, 3, 2, 96), f32),
            pltpu.VMEM((4, 3, 2, 96), f32),
            pltpu.VMEM((4, 3, 2, 96), f32),
            pltpu.VMEM((4, 1, 48), f32),
            pltpu.VMEM((6, 9, CH, CH), bf16),
            pltpu.VMEM((9, CH, UP), bf16),
            pltpu.VMEM((24, CH), f32),
            pltpu.VMEM((3, 288, 128), bf16),
            pltpu.VMEM((144, CH), bf16),
            pltpu.VMEM((2, 16, COLS, 3 * CH), bf16),
            pltpu.VMEM((16, COLS, CH), f32),
            pltpu.VMEM((2, 2, 128, 128), f32),
            pltpu.VMEM((4, UP, 128), bf16),
            dma((36,)),
            dma((36,)),
            dma((24,)),
            dma((24,)),
            dma((18,)),
            dma((NPIECE,)),
            dma((NPIECE,)),
            dma((NPIECE,)),
            dma((NPIECE,)),
            dma((NPIECE,)),
            dma((NPIECE,)),
            dma((16,)),
            dma((16,)),
        ],
        compiler_params=pltpu.CompilerParams(
            collective_id=0, has_side_effects=True, vmem_limit_bytes=60 << 20
        ),
    )(
        latent.T,
        in_weight.reshape(36, CH),
        in_bias[None],
        norm_gain,
        norm_shift,
        res_weight,
        res_bias,
        up_weight,
        up_bias[None],
    )
    return image.transpose(1, 0, 2)


def solution(mesh):
    placed = (
        P(("seq", "chan"), None),
        P(None, "chan", None),
        P("chan"),
        P(None, None, "chan"),
        P(None, None, "chan"),
        P(None, None, None, "chan", None),
        P(None, None, "chan"),
        P(None, "chan", None),
        P("chan"),
    )
    return jax.shard_map(
        body, mesh=mesh, in_specs=placed, out_specs=P("chan", "seq", None), check_vma=False
    )
```

```python
import jax
import jax.numpy as jnp
from jax import lax
from jax.experimental import pallas as pl
from jax.experimental.pallas import tpu as pltpu
from jax.sharding import PartitionSpec as P

CH = 384
UP = 192
EPS = 1e-06
COLS = 80
NRES = 54
NPIECE = 63
LAG = 14
SHORT = frozenset(range(45, 63))
FIRST = 12
MESH = pl.DeviceIdType.MESH


def remote(src, dst, send_sem, recv_sem, device):
    return pltpu.make_async_remote_copy(
        src_ref=src,
        dst_ref=dst,
        send_sem=send_sem,
        recv_sem=recv_sem,
        device_id=device,
        device_id_type=MESH,
    )


def kernel(
    lat_in, win_in, ibias_in, gain_in, shift_in, wres_in, rbias_in, wup_in, ubias_in,
    out_ref,
    lat_buf, win_buf, ibias_buf, gain_buf, shift_buf, rbias_buf, ubias_buf,
    wbuf, ubuf, table, lrow, wide, win, x3, hbuf, acc, upx, obuf,
    lat_s, lat_r, small_s, small_r, loc, zs, xs, ys, ps, r1, r2, out_s, out_r,
):
    s = lax.axis_index("seq")
    c = lax.axis_index("chan")
    core = lax.rem(s, 2)
    x = lax.rem(lax.div(s, 2), 4)
    y = lax.rem(lax.div(s, 8), 8)
    zh = lax.div(s, 64)
    z = zh * 4 + c
    bx, by = lax.rem(x, 2), lax.rem(y, 2)
    partner = (s + 1 - 2 * core, c)

    def z_device(step):
        zz = lax.rem(z + 8 + step, 8)
        return (((lax.div(zz, 4) * 8 + y) * 4 + x) * 2 + core, lax.rem(zz, 4))

    def x_device(step):
        xx = lax.rem(x + 4 + step, 4)
        return (((zh * 8 + y) * 4 + xx) * 2 + core, c)

    def y_device(step):
        yy = lax.rem(y + 8 + step, 8)
        return (((zh * 8 + yy) * 4 + x) * 2 + core, c)

    barrier = pltpu.get_barrier_semaphore()
    others = []
    for ds in range(-4, 5):
        peer = lax.rem(s + 128 + ds, 128)
        for dc in range(4):
            if ds != 0 or dc != 0:
                others.append((peer, lax.rem(c + dc, 4)))
    for step in (-2, -1, 1, 2):
        others.append(z_device(step))
    for step in (-1, 1):
        others.append(x_device(step))
        others.append(y_device(step))
    for device in others:
        pl.semaphore_signal(barrier, inc=1, device_id=device, device_id_type=MESH)
    for k in range(6):
        pltpu.make_async_copy(
            wres_in.at[k // 2, k % 2], wbuf.at[k, :, pl.ds(c * 96, 96), :], loc.at[k]
        ).start()
    pltpu.make_async_copy(wup_in, ubuf.at[:, pl.ds(c * 96, 96), :], loc.at[6]).start()
    pl.semaphore_wait(barrier, len(others))

    def lat_copy(ds, dc):
        return remote(
            lat_in,
            lat_buf.at[4 * (4 - ds) + c],
            lat_s.at[(ds + 4) * 4 + dc],
            lat_r.at[4 * (4 - ds) + c],
            (lax.rem(s + 128 + ds, 128), lax.rem(c + dc, 4)),
        )

    lat_pairs = [(ds, dc) for ds in range(-4, 5) for dc in range(4) if ds != 0 or dc != 0]
    for ds, dc in lat_pairs:
        lat_copy(ds, dc).start()
    pltpu.make_async_copy(lat_in, lat_buf.at[16 + c], loc.at[7]).start()
    smalls = (
        (win_in, win_buf),
        (ibias_in, ibias_buf),
        (gain_in, gain_buf),
        (shift_in, shift_buf),
        (rbias_in, rbias_buf),
        (ubias_in, ubias_buf),
    )

    def small_copy(i, dc):
        src, dst = smalls[i]
        return remote(
            src, dst.at[c], small_s.at[i * 4 + dc], small_r.at[i * 4 + c], (s, lax.rem(c + dc, 4))
        )

    for i in range(6):
        for dc in range(1, 4):
            small_copy(i, dc).start()
        pltpu.make_async_copy(smalls[i][0], smalls[i][1].at[c], loc.at[8 + i]).start()

    sign = 1 - 2 * core
    hops = {step: z_device(step * sign) for step in (-2, -1, 1, 2)}
    aside = {step: x_device(step * sign) for step in (-1, 1)}
    along = {step: y_device(step * sign) for step in (-1, 1)}
    mine = [lax.rem(c + 4 + q * sign, 4) * 96 + core * 48 for q in range(4)]
    theirs = [lax.rem(c + 4 - q * sign, 4) * 96 + (1 - core) * 48 for q in range(4)]

    def piece_at(v, row):
        if v < NRES:
            return wbuf.at[v // 9, pl.ds(v % 9 // 3 * 3, 3), pl.ds(row, 48), :]
        return ubuf.at[pl.ds((v - NRES) // 3 * 3, 3), pl.ds(row, 48), :]

    def source_copy(v):
        step = (-1, 4 * (v // 12 % 2) - 2, 1)[v % 3]
        rows = pl.ds(core * 48, 48)
        if v < NRES:
            src = wres_in.at[v // 18, v // 9 % 2, pl.ds(v % 9 // 3 * 3, 3), rows, :]
        else:
            src = wup_in.at[pl.ds((v - NRES) // 3 * 3, 3), rows, :]
        return remote(src, piece_at(v, mine[0]), zs.at[v], r1.at[v], hops[step])

    def is_colour(i):
        return (bx == i % 2) & (by == i // 2)

    def x_is_last(v):
        return v // 4 % 2 == 1

    def is_source(v):
        if v in SHORT:
            return bx == v % 2 if x_is_last(v) else by == v // 2 % 2
        return is_colour(v % 4)

    for v in range(NPIECE):

        @pl.when(is_source(v))
        def _():
            source_copy(v).start()

    def x_copy(v):
        piece = piece_at(v, mine[1 + v % 3])
        return remote(piece, piece, xs.at[v], r1.at[v], aside[2 * (v // 8 % 2) - 1])

    def y_copy(v):
        piece = piece_at(v, mine[1 + v % 3])
        return remote(piece, piece, ys.at[v], r1.at[v], along[2 * (v // 8 % 2) - 1])

    def core_copy(v):
        piece = piece_at(v, mine[1 + v % 3])
        return remote(piece, piece, ps.at[v], r2.at[v], partner)

    def phases(v):
        final = x_copy if x_is_last(v) else y_copy
        rest = bx != v % 2 if x_is_last(v) else by != v // 2 % 2
        if v in SHORT:
            return ((is_source(v), (final,)), (rest, ()))
        second = is_colour(v % 4 ^ (2 if x_is_last(v) else 1))
        return ((is_source(v), (x_copy, y_copy)), (second, (final,)), (rest, ()))

    def length(v):
        return 2 if v in SHORT else 3

    def relay(t):
        for phase in range(3):
            v = t - LAG * phase
            if 0 <= v < NPIECE and phase < length(v):
                reached, onward = phases(v)[phase]

                @pl.when(reached)
                def _():
                    x_copy(v).wait_recv()
                    for copy in onward:
                        copy(v).start()
                    core_copy(v).start()

    def relays(lo, hi):
        for t in range(lo, hi):
            relay(t)

    def arrived(v):
        piece = piece_at(v, theirs[1 + v % 3])
        remote(piece, piece, ps.at[v], r2.at[v], partner).wait_recv()

    need = [
        1 + max(v + LAG * (length(v) - 1) for v in range(9 * k + 9)) for k in range(7)
    ]
    relays(0, FIRST)

    for i in range(6):
        for dc in range(1, 4):
            src, dst = smalls[i]
            peer = lax.rem(c + dc, 4)
            remote(
                src, dst.at[peer], small_s.at[i * 4 + dc], small_r.at[i * 4 + peer], (s, peer)
            ).wait_recv()
        pltpu.make_async_copy(smalls[i][0], smalls[i][1].at[c], loc.at[8 + i]).wait()
    for q in range(4):
        for i in range(6):
            at = pl.ds(96 * q, 96)
            table[pl.ds(i, 1), at] = gain_buf[q, i // 2, pl.ds(i % 2, 1), :]
            table[pl.ds(6 + i, 1), at] = shift_buf[q, i // 2, pl.ds(i % 2, 1), :]
            table[pl.ds(12 + i, 1), at] = rbias_buf[q, i // 2, pl.ds(i % 2, 1), :]
        table[pl.ds(18, 1), pl.ds(96 * q, 96)] = ibias_buf[q]
        table[pl.ds(19, 1), pl.ds(48 * q, 48)] = ubias_buf[q]
    for q in range(4):
        for t in range(9):
            wide[pl.ds(16 * t + 4 * q, 4), :] = win_buf[q, t].astype(jnp.float32)
    win[...] = wide[...].astype(jnp.bfloat16)

    for ds, dc in lat_pairs:
        slot = 4 * (4 - ds) + lax.rem(c + dc, 4)
        remote(lat_in, lat_buf.at[slot], lat_s.at[0], lat_r.at[slot], partner).wait_recv()
    pltpu.make_async_copy(lat_in, lat_buf.at[16 + c], loc.at[7]).wait()
    col_lo = jnp.maximum(8 - 64 * c, 0)
    col_hi = jnp.minimum(264 - 64 * c, COLS)
    turn = lax.rem(8 + 256 - 64 * c, 256)
    lane = lax.broadcasted_iota(jnp.int32, (16, 128), 1)

    @pl.loop(0, 18)
    def _(r):
        both = jnp.concatenate([lat_buf[2 * r], lat_buf[2 * r + 1]], axis=1).astype(jnp.float32)
        window = pltpu.roll(both, turn, 1)[:, :128]
        row = 2 * s - 8 + r
        top = jnp.where((row >= 0) & (row < 256), col_hi, 0)
        window = jnp.where((lane >= col_lo) & (lane < top), window, 0.0)
        at = pl.ds(pl.multiple_of(r * 16, 16), 16)
        lrow[0, at, :] = pltpu.roll(window, 1, 1).astype(jnp.bfloat16)
        lrow[1, at, :] = window.astype(jnp.bfloat16)
        lrow[2, at, :] = pltpu.roll(window, 127, 1).astype(jnp.bfloat16)

    pixel = lax.broadcasted_iota(jnp.int32, (COLS, CH), 0)

    def spread(dst, a, values):
        row = 2 * s - 7 + a
        top = jnp.where((row >= 0) & (row < 256), col_hi, 0)
        kept = jnp.where((pixel >= col_lo) & (pixel < top), values, 0.0)
        x3[dst, a, :, pl.ds(0, CH)] = pltpu.roll(kept, 1, 0).astype(jnp.bfloat16)
        x3[dst, a, :, pl.ds(CH, CH)] = kept.astype(jnp.bfloat16)
        x3[dst, a, :, pl.ds(2 * CH, CH)] = pltpu.roll(kept, COLS - 1, 0).astype(jnp.bfloat16)

    def normed(values, i):
        mean = jnp.sum(values * values, axis=1, keepdims=True) * (1.0 / CH)
        u = values * lax.rsqrt(mean + EPS) * table[pl.ds(i, 1), :] + table[pl.ds(6 + i, 1), :]
        half = 0.5 * u
        return half * jnp.tanh(half) + half

    def rounded(values):
        return values.astype(jnp.bfloat16).astype(jnp.float32)

    def first_conv(i):
        columns = jnp.concatenate(
            [
                lrow[q, pl.ds(pl.multiple_of((i + p) * 16, 16), 16), :]
                for p in range(3)
                for q in range(3)
            ],
            axis=0,
        )
        product = lax.dot_general(
            columns, win[...], (((0,), (0,)), ((), ())), preferred_element_type=jnp.float32
        )
        stream = rounded(product[:COLS] + table[pl.ds(18, 1), :])
        hbuf[i] = stream
        spread(0, i, normed(stream, 0))

    for part in range(4):
        pl.loop(4 * part, 4 * part + 4)(first_conv)
        relays(FIRST + part * (need[0] - FIRST) // 4, FIRST + (part + 1) * (need[0] - FIRST) // 4)

    for k in range(6):
        src, dst = k % 2, 1 - k % 2
        pltpu.make_async_copy(
            wres_in.at[k // 2, k % 2], wbuf.at[k, :, pl.ds(c * 96, 96), :], loc.at[k]
        ).wait()

        for v in range(9 * k, 9 * k + 9):
            arrived(v)
        height = 7 - k
        done, steps = need[k], need[k + 1] - need[k]

        @pl.loop(0, 2)
        def _(b):
            a = k + 1 + height * b
            sums = acc.at[pl.ds(0, height * COLS)]

            def keep_on(p):
                for part in range(2):

                    @pl.when(b == part)
                    def _():
                        at = 3 * part + p
                        relays(done + steps * at // 6, done + steps * (at + 1) // 6)

            for p in range(3):
                term = jnp.dot(
                    x3[src, pl.ds(a - 1 + p, height)].reshape(height * COLS, 3 * CH),
                    wbuf[k, pl.ds(3 * p, 3)].reshape(3 * CH, CH),
                    preferred_element_type=jnp.float32,
                )
                if p == 0:
                    sums[...] = term
                elif p == 1:
                    sums[...] += term
                if p < 2:
                    keep_on(p)
            total = sums[...] + term + table[pl.ds(12 + k, 1), :]
            for j in range(height):
                values = total[j * COLS : (j + 1) * COLS]
                if k % 2 == 0:
                    spread(dst, a + j, normed(values, k + 1))
                else:
                    values = rounded(hbuf[a + j] + values)
                    hbuf[a + j] = values
                    spread(dst, a + j, normed(values, k + 1) if k < 5 else values)
            keep_on(2)

    pltpu.make_async_copy(wup_in, ubuf.at[:, pl.ds(c * 96, 96), :], loc.at[6]).wait()

    for v in range(NRES, NPIECE):
        arrived(v)

    def out_copy(r, dc):
        peer = lax.rem(c + dc, 4)
        return remote(
            obuf.at[r, pl.ds(peer * 48, 48), :],
            out_ref.at[r, :, pl.ds(c * 128, 128)],
            out_s.at[r * 4 + dc],
            out_r.at[r * 4 + c],
            (s, peer),
        )

    lanes = ((0, 1, 1), (1, 1, 2))
    rows = ((-1, 0, 0), (0, 0, 1))
    for i in range(2):
        for b2 in range(2):
            grown = jnp.zeros((2 * COLS, UP), jnp.float32)
            for p in range(3):
                lhs = jnp.concatenate(
                    [
                        jnp.concatenate(
                            [
                                x3[0, 7 + i + rows[a2][p], :, pl.ds(CH * lanes[b2][q], CH)]
                                for q in range(3)
                            ],
                            axis=1,
                        )
                        for a2 in range(2)
                    ],
                    axis=0,
                )
                grown += jnp.dot(
                    lhs,
                    ubuf[pl.ds(3 * p, 3)].reshape(3 * CH, UP),
                    preferred_element_type=jnp.float32,
                )
            grown += table[pl.ds(19, 1), pl.ds(0, UP)]
            for a2 in range(2):
                part = grown[a2 * COLS + 8 : a2 * COLS + 72]
                upx[a2, 0, pl.ds(b2, 64, stride=2), :] = part[:, :128]
                upx[a2, 1, pl.ds(b2, 64, stride=2), pl.ds(0, 64)] = part[:, 128:]
        for a2 in range(2):
            r = 2 * i + a2
            obuf[r, pl.ds(0, 128), :] = upx[a2, 0].T.astype(jnp.bfloat16)
            obuf[r, pl.ds(128, 64), :] = upx[a2, 1].T[:64].astype(jnp.bfloat16)
            for dc in range(1, 4):
                out_copy(r, dc).start()
            pltpu.make_async_copy(
                obuf.at[r, pl.ds(c * 48, 48), :],
                out_ref.at[r, :, pl.ds(c * 128, 128)],
                loc.at[14 + r],
            ).start()

    for v in range(NPIECE):

        @pl.when(is_source(v))
        def _():
            source_copy(v).wait_send()

        for reached, onward in phases(v)[:-1]:

            @pl.when(reached)
            def _():
                for copy in onward:
                    copy(v).wait_send()

        core_copy(v).wait_send()
    for ds, dc in lat_pairs:
        lat_copy(ds, dc).wait_send()
    for i in range(6):
        for dc in range(1, 4):
            small_copy(i, dc).wait_send()
    for r in range(4):
        for dc in range(1, 4):
            out_copy(r, dc).wait_send()
            peer = lax.rem(c + dc, 4)
            remote(
                obuf.at[r, pl.ds(0, 48), :],
                out_ref.at[r, :, pl.ds(peer * 128, 128)],
                out_s.at[r * 4 + dc],
                out_r.at[r * 4 + peer],
                (s, peer),
            ).wait_recv()
        pltpu.make_async_copy(
            obuf.at[r, pl.ds(c * 48, 48), :],
            out_ref.at[r, :, pl.ds(c * 128, 128)],
            loc.at[14 + r],
        ).wait()


def body(
    latent, in_weight, in_bias, norm_gain, norm_shift, res_weight, res_bias, up_weight, up_bias
):
    bf16, f32 = jnp.bfloat16, jnp.float32
    dma = pltpu.SemaphoreType.DMA
    image = pl.pallas_call(
        kernel,
        out_shape=jax.ShapeDtypeStruct((4, 48, 512), bf16),
        in_specs=[pl.BlockSpec(memory_space=pl.ANY)] * 9,
        out_specs=pl.BlockSpec(memory_space=pltpu.VMEM),
        scratch_shapes=[
            pltpu.VMEM((36, 16, 128), bf16),
            pltpu.VMEM((4, 9, 4, CH), bf16),
            pltpu.VMEM((4, 1, 96), f32),
            pltpu.VMEM((4, 3, 2, 96), f32),
            pltpu.VMEM((4, 3, 2, 96), f32),
            pltpu.VMEM((4, 3, 2, 96), f32),
            pltpu.VMEM((4, 1, 48), f32),
            pltpu.VMEM((6, 9, CH, CH), bf16),
            pltpu.VMEM((9, CH, UP), bf16),
            pltpu.VMEM((24, CH), f32),
            pltpu.VMEM((3, 288, 128), bf16),
            pltpu.VMEM((144, CH), f32),
            pltpu.VMEM((144, CH), bf16),
            pltpu.VMEM((2, 16, COLS, 3 * CH), bf16),
            pltpu.VMEM((16, COLS, CH), f32),
            pltpu.VMEM((7 * COLS, CH), f32),
            pltpu.VMEM((2, 2, 128, 128), f32),
            pltpu.VMEM((4, UP, 128), bf16),
            dma((36,)),
            dma((36,)),
            dma((24,)),
            dma((24,)),
            dma((18,)),
            dma((NPIECE,)),
            dma((NPIECE,)),
            dma((NPIECE,)),
            dma((NPIECE,)),
            dma((NPIECE,)),
            dma((NPIECE,)),
            dma((16,)),
            dma((16,)),
        ],
        compiler_params=pltpu.CompilerParams(
            collective_id=0, has_side_effects=True, vmem_limit_bytes=60 << 20
        ),
    )(
        latent.T,
        in_weight,
        in_bias[None],
        norm_gain,
        norm_shift,
        res_weight,
        res_bias,
        up_weight,
        up_bias[None],
    )
    return image.transpose(1, 0, 2)


def solution(mesh):
    placed = (
        P(("seq", "chan"), None),
        P(None, "chan", None),
        P("chan"),
        P(None, None, "chan"),
        P(None, None, "chan"),
        P(None, None, None, "chan", None),
        P(None, None, "chan"),
        P(None, "chan", None),
        P("chan"),
    )
    return jax.shard_map(
        body, mesh=mesh, in_specs=placed, out_specs=P("chan", "seq", None), check_vma=False
    )
```

```python
import jax
import jax.numpy as jnp
from jax import lax
from jax.experimental import pallas as pl
from jax.experimental.pallas import tpu as pltpu
from jax.sharding import PartitionSpec as P

CH = 384
UP = 192
EPS = 1e-06
COLS = 80
NRES = 54
NPIECE = 63
LAGS = tuple(min(14, 7 + v // 6) for v in range(63))
SHORT = frozenset(range(45, 63))
FIRST = 10
MESH = pl.DeviceIdType.MESH


def remote(src, dst, send_sem, recv_sem, device):
    return pltpu.make_async_remote_copy(
        src_ref=src,
        dst_ref=dst,
        send_sem=send_sem,
        recv_sem=recv_sem,
        device_id=device,
        device_id_type=MESH,
    )


def kernel(
    lat_in, win_in, ibias_in, gain_in, shift_in, wres_in, rbias_in, wup_in, ubias_in,
    out_ref,
    lat_buf, win_buf, ibias_buf, gain_buf, shift_buf, rbias_buf, ubias_buf,
    wbuf, ubuf, table, lrow, wide, win, x3, hbuf, acc, upx, obuf,
    lat_s, lat_r, small_s, small_r, loc, zs, xs, ys, ps, r1, r2, out_s, out_r,
):
    s = lax.axis_index("seq")
    c = lax.axis_index("chan")
    core = lax.rem(s, 2)
    x = lax.rem(lax.div(s, 2), 4)
    y = lax.rem(lax.div(s, 8), 8)
    zh = lax.div(s, 64)
    z = zh * 4 + c
    bx, by = lax.rem(x, 2), lax.rem(y, 2)
    partner = (s + 1 - 2 * core, c)

    def z_device(step):
        zz = lax.rem(z + 8 + step, 8)
        return (((lax.div(zz, 4) * 8 + y) * 4 + x) * 2 + core, lax.rem(zz, 4))

    def x_device(step):
        xx = lax.rem(x + 4 + step, 4)
        return (((zh * 8 + y) * 4 + xx) * 2 + core, c)

    def y_device(step):
        yy = lax.rem(y + 8 + step, 8)
        return (((zh * 8 + yy) * 4 + x) * 2 + core, c)

    barrier = pltpu.get_barrier_semaphore()
    others = []
    for ds in range(-4, 5):
        peer = lax.rem(s + 128 + ds, 128)
        for dc in range(4):
            if ds != 0 or dc != 0:
                others.append((peer, lax.rem(c + dc, 4)))
    for step in (-2, -1, 1, 2):
        others.append(z_device(step))
    for step in (-1, 1):
        others.append(x_device(step))
        others.append(y_device(step))
    for device in others:
        pl.semaphore_signal(barrier, inc=1, device_id=device, device_id_type=MESH)
    for k in range(6):
        pltpu.make_async_copy(
            wres_in.at[k // 2, k % 2], wbuf.at[k, :, pl.ds(c * 96, 96), :], loc.at[k]
        ).start()
    pltpu.make_async_copy(wup_in, ubuf.at[:, pl.ds(c * 96, 96), :], loc.at[6]).start()
    pl.semaphore_wait(barrier, len(others))

    def lat_copy(ds, dc):
        return remote(
            lat_in,
            lat_buf.at[4 * (4 - ds) + c],
            lat_s.at[(ds + 4) * 4 + dc],
            lat_r.at[4 * (4 - ds) + c],
            (lax.rem(s + 128 + ds, 128), lax.rem(c + dc, 4)),
        )

    lat_pairs = [(ds, dc) for ds in range(-4, 5) for dc in range(4) if ds != 0 or dc != 0]
    for ds, dc in lat_pairs:
        lat_copy(ds, dc).start()
    pltpu.make_async_copy(lat_in, lat_buf.at[16 + c], loc.at[7]).start()
    smalls = (
        (win_in, win_buf),
        (ibias_in, ibias_buf),
        (gain_in, gain_buf),
        (shift_in, shift_buf),
        (rbias_in, rbias_buf),
        (ubias_in, ubias_buf),
    )

    def small_copy(i, dc):
        src, dst = smalls[i]
        return remote(
            src, dst.at[c], small_s.at[i * 4 + dc], small_r.at[i * 4 + c], (s, lax.rem(c + dc, 4))
        )

    for i in range(6):
        for dc in range(1, 4):
            small_copy(i, dc).start()
        pltpu.make_async_copy(smalls[i][0], smalls[i][1].at[c], loc.at[8 + i]).start()

    sign = 1 - 2 * core
    hops = {step: z_device(step * sign) for step in (-2, -1, 1, 2)}
    aside = {step: x_device(step * sign) for step in (-1, 1)}
    along = {step: y_device(step * sign) for step in (-1, 1)}
    mine = [lax.rem(c + 4 + q * sign, 4) * 96 + core * 48 for q in range(4)]
    theirs = [lax.rem(c + 4 - q * sign, 4) * 96 + (1 - core) * 48 for q in range(4)]

    def piece_at(v, row):
        if v < NRES:
            return wbuf.at[v // 9, pl.ds(v % 9 // 3 * 3, 3), pl.ds(row, 48), :]
        return ubuf.at[pl.ds((v - NRES) // 3 * 3, 3), pl.ds(row, 48), :]

    def source_copy(v):
        step = (-1, 4 * (v // 12 % 2) - 2, 1)[v % 3]
        rows = pl.ds(core * 48, 48)
        if v < NRES:
            src = wres_in.at[v // 18, v // 9 % 2, pl.ds(v % 9 // 3 * 3, 3), rows, :]
        else:
            src = wup_in.at[pl.ds((v - NRES) // 3 * 3, 3), rows, :]
        return remote(src, piece_at(v, mine[0]), zs.at[v], r1.at[v], hops[step])

    def is_colour(i):
        return (bx == i % 2) & (by == i // 2)

    def x_is_last(v):
        return v // 4 % 2 == 1

    def is_source(v):
        if v in SHORT:
            return bx == v % 2 if x_is_last(v) else by == v // 2 % 2
        return is_colour(v % 4)

    for v in range(NPIECE):

        @pl.when(is_source(v))
        def _():
            source_copy(v).start()

    def x_copy(v):
        piece = piece_at(v, mine[1 + v % 3])
        return remote(piece, piece, xs.at[v], r1.at[v], aside[2 * (v // 8 % 2) - 1])

    def y_copy(v):
        piece = piece_at(v, mine[1 + v % 3])
        return remote(piece, piece, ys.at[v], r1.at[v], along[2 * (v // 8 % 2) - 1])

    def core_copy(v):
        piece = piece_at(v, mine[1 + v % 3])
        return remote(piece, piece, ps.at[v], r2.at[v], partner)

    def phases(v):
        final = x_copy if x_is_last(v) else y_copy
        rest = bx != v % 2 if x_is_last(v) else by != v // 2 % 2
        if v in SHORT:
            return ((is_source(v), (final,)), (rest, ()))
        second = is_colour(v % 4 ^ (2 if x_is_last(v) else 1))
        return ((is_source(v), (x_copy, y_copy)), (second, (final,)), (rest, ()))

    def length(v):
        return 2 if v in SHORT else 3

    def relay(t):
        for phase in range(3):
            for v in range(NPIECE):
                if v + LAGS[v] * phase != t or phase >= length(v):
                    continue
                reached, onward = phases(v)[phase]

                @pl.when(reached)
                def _():
                    x_copy(v).wait_recv()
                    for copy in onward:
                        copy(v).start()
                    core_copy(v).start()

    def relays(lo, hi):
        for t in range(lo, hi):
            relay(t)

    def arrived(v):
        piece = piece_at(v, theirs[1 + v % 3])
        remote(piece, piece, ps.at[v], r2.at[v], partner).wait_recv()

    need = [
        1 + max(v + LAGS[v] * (length(v) - 1) for v in range(9 * k + 9)) for k in range(7)
    ]
    relays(0, FIRST)

    for i in range(6):
        for dc in range(1, 4):
            src, dst = smalls[i]
            peer = lax.rem(c + dc, 4)
            remote(
                src, dst.at[peer], small_s.at[i * 4 + dc], small_r.at[i * 4 + peer], (s, peer)
            ).wait_recv()
        pltpu.make_async_copy(smalls[i][0], smalls[i][1].at[c], loc.at[8 + i]).wait()
    for q in range(4):
        for i in range(6):
            at = pl.ds(96 * q, 96)
            table[pl.ds(i, 1), at] = gain_buf[q, i // 2, pl.ds(i % 2, 1), :]
            table[pl.ds(6 + i, 1), at] = shift_buf[q, i // 2, pl.ds(i % 2, 1), :]
            table[pl.ds(12 + i, 1), at] = rbias_buf[q, i // 2, pl.ds(i % 2, 1), :]
        table[pl.ds(18, 1), pl.ds(96 * q, 96)] = ibias_buf[q]
        table[pl.ds(19, 1), pl.ds(48 * q, 48)] = ubias_buf[q]
    for q in range(4):
        for t in range(9):
            wide[pl.ds(16 * t + 4 * q, 4), :] = win_buf[q, t].astype(jnp.float32)
    win[...] = wide[...].astype(jnp.bfloat16)

    for ds, dc in lat_pairs:
        slot = 4 * (4 - ds) + lax.rem(c + dc, 4)
        remote(lat_in, lat_buf.at[slot], lat_s.at[0], lat_r.at[slot], partner).wait_recv()
    pltpu.make_async_copy(lat_in, lat_buf.at[16 + c], loc.at[7]).wait()
    col_lo = jnp.maximum(8 - 64 * c, 0)
    col_hi = jnp.minimum(264 - 64 * c, COLS)
    turn = lax.rem(8 + 256 - 64 * c, 256)
    lane = lax.broadcasted_iota(jnp.int32, (16, 128), 1)

    @pl.loop(0, 18)
    def _(r):
        both = jnp.concatenate([lat_buf[2 * r], lat_buf[2 * r + 1]], axis=1).astype(jnp.float32)
        window = pltpu.roll(both, turn, 1)[:, :128]
        row = 2 * s - 8 + r
        top = jnp.where((row >= 0) & (row < 256), col_hi, 0)
        window = jnp.where((lane >= col_lo) & (lane < top), window, 0.0)
        at = pl.ds(pl.multiple_of(r * 16, 16), 16)
        lrow[0, at, :] = pltpu.roll(window, 1, 1).astype(jnp.bfloat16)
        lrow[1, at, :] = window.astype(jnp.bfloat16)
        lrow[2, at, :] = pltpu.roll(window, 127, 1).astype(jnp.bfloat16)

    pixel = lax.broadcasted_iota(jnp.int32, (COLS, CH), 0)

    def spread(dst, a, values):
        row = 2 * s - 7 + a
        top = jnp.where((row >= 0) & (row < 256), col_hi, 0)
        kept = jnp.where((pixel >= col_lo) & (pixel < top), values, 0.0)
        x3[dst, a, :, pl.ds(0, CH)] = pltpu.roll(kept, 1, 0).astype(jnp.bfloat16)
        x3[dst, a, :, pl.ds(CH, CH)] = kept.astype(jnp.bfloat16)
        x3[dst, a, :, pl.ds(2 * CH, CH)] = pltpu.roll(kept, COLS - 1, 0).astype(jnp.bfloat16)

    def normed(values, i):
        mean = jnp.sum(values * values, axis=1, keepdims=True) * (1.0 / CH)
        u = values * lax.rsqrt(mean + EPS) * table[pl.ds(i, 1), :] + table[pl.ds(6 + i, 1), :]
        half = 0.5 * u
        return half * jnp.tanh(half) + half

    def rounded(values):
        return values.astype(jnp.bfloat16).astype(jnp.float32)

    def first_conv(i):
        columns = jnp.concatenate(
            [
                lrow[q, pl.ds(pl.multiple_of((i + p) * 16, 16), 16), :]
                for p in range(3)
                for q in range(3)
            ],
            axis=0,
        )
        product = lax.dot_general(
            columns, win[...], (((0,), (0,)), ((), ())), preferred_element_type=jnp.float32
        )
        stream = rounded(product[:COLS] + table[pl.ds(18, 1), :])
        hbuf[i] = stream
        spread(0, i, normed(stream, 0))

    for part in range(4):
        pl.loop(4 * part, 4 * part + 4)(first_conv)
        relays(FIRST + part * (need[0] - FIRST) // 4, FIRST + (part + 1) * (need[0] - FIRST) // 4)

    for k in range(6):
        src, dst = k % 2, 1 - k % 2
        pltpu.make_async_copy(
            wres_in.at[k // 2, k % 2], wbuf.at[k, :, pl.ds(c * 96, 96), :], loc.at[k]
        ).wait()

        for v in range(9 * k, 9 * k + 9):
            arrived(v)
        height = 7 - k
        done, steps = need[k], need[k + 1] - need[k]

        @pl.loop(0, 2)
        def _(b):
            a = k + 1 + height * b
            sums = acc.at[pl.ds(0, height * COLS)]

            def keep_on(p):
                for part in range(2):

                    @pl.when(b == part)
                    def _():
                        at = 3 * part + p
                        relays(done + steps * at // 6, done + steps * (at + 1) // 6)

            for p in range(3):
                term = jnp.dot(
                    x3[src, pl.ds(a - 1 + p, height)].reshape(height * COLS, 3 * CH),
                    wbuf[k, pl.ds(3 * p, 3)].reshape(3 * CH, CH),
                    preferred_element_type=jnp.float32,
                )
                if p == 0:
                    sums[...] = term
                elif p == 1:
                    sums[...] += term
                if p < 2:
                    keep_on(p)
            total = sums[...] + term + table[pl.ds(12 + k, 1), :]
            for j in range(height):
                values = total[j * COLS : (j + 1) * COLS]
                if k % 2 == 0:
                    spread(dst, a + j, normed(values, k + 1))
                else:
                    values = rounded(hbuf[a + j] + values)
                    hbuf[a + j] = values
                    spread(dst, a + j, normed(values, k + 1) if k < 5 else values)
            keep_on(2)

    pltpu.make_async_copy(wup_in, ubuf.at[:, pl.ds(c * 96, 96), :], loc.at[6]).wait()

    for v in range(NRES, NPIECE):
        arrived(v)

    def out_copy(r, dc):
        peer = lax.rem(c + dc, 4)
        return remote(
            obuf.at[r, pl.ds(peer * 48, 48), :],
            out_ref.at[r, :, pl.ds(c * 128, 128)],
            out_s.at[r * 4 + dc],
            out_r.at[r * 4 + c],
            (s, peer),
        )

    lanes = ((0, 1, 1), (1, 1, 2))
    rows = ((-1, 0, 0), (0, 0, 1))
    for i in range(2):
        for b2 in range(2):
            grown = jnp.zeros((2 * COLS, UP), jnp.float32)
            for p in range(3):
                lhs = jnp.concatenate(
                    [
                        jnp.concatenate(
                            [
                                x3[0, 7 + i + rows[a2][p], :, pl.ds(CH * lanes[b2][q], CH)]
                                for q in range(3)
                            ],
                            axis=1,
                        )
                        for a2 in range(2)
                    ],
                    axis=0,
                )
                grown += jnp.dot(
                    lhs,
                    ubuf[pl.ds(3 * p, 3)].reshape(3 * CH, UP),
                    preferred_element_type=jnp.float32,
                )
            grown += table[pl.ds(19, 1), pl.ds(0, UP)]
            for a2 in range(2):
                part = grown[a2 * COLS + 8 : a2 * COLS + 72]
                upx[a2, 0, pl.ds(b2, 64, stride=2), :] = part[:, :128]
                upx[a2, 1, pl.ds(b2, 64, stride=2), pl.ds(0, 64)] = part[:, 128:]
        for a2 in range(2):
            r = 2 * i + a2
            obuf[r, pl.ds(0, 128), :] = upx[a2, 0].T.astype(jnp.bfloat16)
            obuf[r, pl.ds(128, 64), :] = upx[a2, 1].T[:64].astype(jnp.bfloat16)
            for dc in range(1, 4):
                out_copy(r, dc).start()
            pltpu.make_async_copy(
                obuf.at[r, pl.ds(c * 48, 48), :],
                out_ref.at[r, :, pl.ds(c * 128, 128)],
                loc.at[14 + r],
            ).start()

    for v in range(NPIECE):

        @pl.when(is_source(v))
        def _():
            source_copy(v).wait_send()

        for reached, onward in phases(v)[:-1]:

            @pl.when(reached)
            def _():
                for copy in onward:
                    copy(v).wait_send()

        core_copy(v).wait_send()
    for ds, dc in lat_pairs:
        lat_copy(ds, dc).wait_send()
    for i in range(6):
        for dc in range(1, 4):
            small_copy(i, dc).wait_send()
    for r in range(4):
        for dc in range(1, 4):
            out_copy(r, dc).wait_send()
            peer = lax.rem(c + dc, 4)
            remote(
                obuf.at[r, pl.ds(0, 48), :],
                out_ref.at[r, :, pl.ds(peer * 128, 128)],
                out_s.at[r * 4 + dc],
                out_r.at[r * 4 + peer],
                (s, peer),
            ).wait_recv()
        pltpu.make_async_copy(
            obuf.at[r, pl.ds(c * 48, 48), :],
            out_ref.at[r, :, pl.ds(c * 128, 128)],
            loc.at[14 + r],
        ).wait()


def body(
    latent, in_weight, in_bias, norm_gain, norm_shift, res_weight, res_bias, up_weight, up_bias
):
    bf16, f32 = jnp.bfloat16, jnp.float32
    dma = pltpu.SemaphoreType.DMA
    image = pl.pallas_call(
        kernel,
        out_shape=jax.ShapeDtypeStruct((4, 48, 512), bf16),
        in_specs=[pl.BlockSpec(memory_space=pl.ANY)] * 9,
        out_specs=pl.BlockSpec(memory_space=pltpu.VMEM),
        scratch_shapes=[
            pltpu.VMEM((36, 16, 128), bf16),
            pltpu.VMEM((4, 9, 4, CH), bf16),
            pltpu.VMEM((4, 1, 96), f32),
            pltpu.VMEM((4, 3, 2, 96), f32),
            pltpu.VMEM((4, 3, 2, 96), f32),
            pltpu.VMEM((4, 3, 2, 96), f32),
            pltpu.VMEM((4, 1, 48), f32),
            pltpu.VMEM((6, 9, CH, CH), bf16),
            pltpu.VMEM((9, CH, UP), bf16),
            pltpu.VMEM((24, CH), f32),
            pltpu.VMEM((3, 288, 128), bf16),
            pltpu.VMEM((144, CH), f32),
            pltpu.VMEM((144, CH), bf16),
            pltpu.VMEM((2, 16, COLS, 3 * CH), bf16),
            pltpu.VMEM((16, COLS, CH), f32),
            pltpu.VMEM((7 * COLS, CH), f32),
            pltpu.VMEM((2, 2, 128, 128), f32),
            pltpu.VMEM((4, UP, 128), bf16),
            dma((36,)),
            dma((36,)),
            dma((24,)),
            dma((24,)),
            dma((18,)),
            dma((NPIECE,)),
            dma((NPIECE,)),
            dma((NPIECE,)),
            dma((NPIECE,)),
            dma((NPIECE,)),
            dma((NPIECE,)),
            dma((16,)),
            dma((16,)),
        ],
        compiler_params=pltpu.CompilerParams(
            collective_id=0, has_side_effects=True, vmem_limit_bytes=60 << 20
        ),
    )(
        latent.T,
        in_weight,
        in_bias[None],
        norm_gain,
        norm_shift,
        res_weight,
        res_bias,
        up_weight,
        up_bias[None],
    )
    return image.transpose(1, 0, 2)


def solution(mesh):
    placed = (
        P(("seq", "chan"), None),
        P(None, "chan", None),
        P("chan"),
        P(None, None, "chan"),
        P(None, None, "chan"),
        P(None, None, None, "chan", None),
        P(None, None, "chan"),
        P(None, "chan", None),
        P("chan"),
    )
    return jax.shard_map(
        body, mesh=mesh, in_specs=placed, out_specs=P("chan", "seq", None), check_vma=False
    )
```
